256 devices in a mesh: shot: 16 (over x_lo, y, core), rbin: 16 (over x_hi, z).
Axes of the slice: x: 4 (x_hi: 2, x_lo: 2; x = x_hi * 2 + x_lo), y: 4, z: 8, core: 2. Of those that a mesh axis runs over, the one named last changes fastest.
Arguments:
- local_gathers: bfloat16 [2, 2, 8192, 4096], P(None, None, 'shot', 'rbin'), may hold values from -6 to 6
- recorded_shots: bfloat16 [16, 2, 2, 1024, 2048], P('shot', None, None, 'rbin'), may hold values from -0.125 to 0.125
- block_owner: int32 [4], replicated, may hold values from 0 to 15, as said below
- aperture_start: int32 [8192], P('shot'), may hold values from 0 to 4095, as said below
- aperture_end: int32 [8192], P('shot'), may hold values from 1 to 4096
- taper_bin: int32 [4096], P('rbin'), may hold values from 0 to 7
- taper_gain: float32 [8], replicated, may hold values from 0.25 to 1
Outputs:
- multiples: float32 [2, 2048, 2, 8192], P(None, 'rbin', None, 'shot')
The draws below stay inside these ranges and needn't reach their ends.
Inputs may be any that keep to these rules, and one draw needn't show every extreme that they name: `block_owner`: the 4 entries are distinct. aperture_start < aperture_end for every shot.
All inputs are finite; a program needn't handle non-finite values.
Results may differ from the reference program's by a relative error of at most 0.0029.
Values may be sent and summed in bfloat16 or wider, within the bound.
A program may use at most 128 MiB of HBM per device.

```python
import jax
import jax.numpy as jnp
from jax import lax

RECEIVERS = 2048
FREQS = 2
BLOCKS = 4
TAPER_BINS = 8
SHOTS = 8192
POINTS = 4096
BLOCK_POINTS = 64
EDGE = 64
SLOTS = 16
N_RBIN = 16


def aperture_pair(key):
    centre_point = jax.random.randint(jax.random.fold_in(key, 11), (SHOTS,), 0, POINTS)
    half_width = jax.random.randint(jax.random.fold_in(key, 12), (SHOTS,), POINTS // 16, POINTS // 4 + 1)
    starting = jnp.maximum(centre_point - half_width, 0)
    ending = jnp.minimum(centre_point + half_width, POINTS)
    starting = starting.at[0].set(0)
    ending = ending.at[SHOTS - 1].set(POINTS)
    starting = starting.at[1].set(0)
    ending = ending.at[1].set(1)
    starting = starting.at[SHOTS - 2].set(POINTS - 1)
    ending = ending.at[SHOTS - 2].set(POINTS)
    return (starting.astype(jnp.int32), ending.astype(jnp.int32))


def draw_aperture_start(key, part):
    return aperture_pair(key)[0]


def draw_aperture_end(key, part):
    return aperture_pair(key)[1]


def draw_block_owner(key, part):
    middle = 1 + jax.random.permutation(jax.random.fold_in(key, 21), SLOTS - 2)[:BLOCKS - 2]
    endings = jnp.array([0, SLOTS - 1], jnp.int32)
    together = jnp.concatenate([endings, middle.astype(jnp.int32)])
    return jax.random.permutation(jax.random.fold_in(key, 22), together).astype(jnp.int32)


def touch_ends(entries, stream_key, least, largest):
    longest = entries.shape.index(max(entries.shape))
    spots = []
    for shift in (0, 1):
        where = [jax.random.randint(jax.random.fold_in(stream_key, axis), (), 0, length) for axis, length in enumerate(entries.shape)]
        where[longest] = (where[longest] + shift) % entries.shape[longest]
        spots.append(tuple(where))
    return entries.at[spots[0]].set(least).at[spots[1]].set(largest)


def spiked(values, key, source, target, parts, factor):
    def block_of(position):
        return (jnp.arange(values.shape[position]) // (values.shape[position] // parts)).reshape((-1,) + (1,) * (values.ndim - 1 - position))

    one_side = jax.random.permutation(key, parts)[block_of(target)]
    second = (block_of(target) + parts // 2) % parts
    return jnp.where((block_of(source) == one_side) | (block_of(source) == second), factor * values, values)


def shard_levels(key, extent, split, least, largest):
    def one(dim, parts):
        draws = jax.random.uniform(jax.random.fold_in(jax.random.fold_in(key, 6), dim), (parts,), jnp.float32, least / len(split), largest / len(split))
        return jnp.repeat(jnp.exp(draws), extent[dim] // parts).reshape((-1,) + (1,) * (len(extent) - dim - 1))

    factor_of = one(*split[0])
    for cut in split[1:]:
        factor_of = factor_of * one(*cut)
    return factor_of


def normal_values(stream_key, extent, scale, most, cuts=(), kind=jnp.bfloat16):
    loudness = shard_levels(stream_key, extent, cuts, -0.22, 0.18) if cuts else 1.0
    values = jax.random.normal(stream_key, extent, jnp.float32) * scale * loudness
    return jnp.minimum(jnp.maximum(values, -most), most).astype(kind)


def bell_draw_with(key, dims, width, most, cuts, heavy, kind=jnp.bfloat16):
    values = width * jax.random.normal(key, dims, jnp.float32)
    if cuts:
        values = values * shard_levels(key, dims, cuts, -0.22, 0.18)
    return jnp.clip(spiked(values, jax.random.fold_in(key, 3), *heavy), -most, most).astype(kind)


def setup_inputs(seed: int = 0) -> dict:
    splits = jax.random.split(jax.random.key(seed), 8)
    local_gathers = normal_values(splits[0], (FREQS, 2, SHOTS, POINTS), 1.0, 6.0, ((2, 16), (3, 16)))
    recorded_shots = bell_draw_with(splits[1], (SLOTS, FREQS, 2, BLOCK_POINTS * N_RBIN, RECEIVERS), POINTS ** -0.5, 0.125, ((0, 16), (3, 16)), (3, 4, 16, 2.0))
    block_owner = draw_block_owner(jax.random.fold_in(splits[7], 71), 0)
    aperture_start = draw_aperture_start(jax.random.fold_in(splits[7], 71), 0)
    aperture_end = draw_aperture_end(jax.random.fold_in(splits[7], 71), 0)
    taper_bin = touch_ends(jax.random.randint(splits[5], (POINTS,), 0, TAPER_BINS), jax.random.fold_in(splits[5], 1), 0, TAPER_BINS - 1).astype(jnp.int32)
    taper_gain = jnp.clip(jax.random.uniform(splits[6], (TAPER_BINS,), jnp.float32, 0.25, 1.0), 0.25, 1.0)
    return {"local_gathers": local_gathers, "recorded_shots": recorded_shots, "block_owner": block_owner, "aperture_start": aperture_start, "aperture_end": aperture_end, "taper_bin": taper_bin, "taper_gain": taper_gain}


def taper_weights(aperture_start, aperture_end, taper_bin, taper_gain):
    columns = jnp.arange(POINTS, dtype=jnp.int32)
    inside = (columns[None, :] >= aperture_start[:, None]) & (columns[None, :] < aperture_end[:, None])
    distance = jnp.minimum(columns[None, :] - aperture_start[:, None], aperture_end[:, None] - 1 - columns[None, :])
    ramped = jnp.minimum((distance + 1).astype(jnp.float32) / EDGE, 1.0)
    return jnp.where(inside, ramped, 0.0) * taper_gain[taper_bin][None, :]


def reference(local_gathers, recorded_shots, block_owner, aperture_start, aperture_end, taper_bin, taper_gain):
    weight = taper_weights(aperture_start, aperture_end, taper_bin, taper_gain)
    tapered = (local_gathers.astype(jnp.float32) * weight[None, None]).astype(jnp.bfloat16)
    grouped = tapered.reshape(FREQS, 2, SHOTS, N_RBIN, BLOCKS, BLOCK_POINTS)
    accumulated = jnp.zeros((FREQS, RECEIVERS, 2, SHOTS), jnp.float32)
    for block_index in range(BLOCKS):
        received = lax.dynamic_index_in_dim(recorded_shots, block_owner[block_index], 0, keepdims=False).astype(jnp.float32)
        picked = grouped[:, :, :, :, block_index, :].reshape(FREQS, 2, SHOTS, N_RBIN * BLOCK_POINTS).astype(jnp.float32)
        real_part = jnp.einsum("fsx,fxr->frs", picked[:, 0], received[:, 0]) - jnp.einsum("fsx,fxr->frs", picked[:, 1], received[:, 1])
        imag_part = jnp.einsum("fsx,fxr->frs", picked[:, 0], received[:, 1]) + jnp.einsum("fsx,fxr->frs", picked[:, 1], received[:, 0])
        accumulated = accumulated + jnp.stack([real_part, imag_part], axis=2)
    return -accumulated
```

```python
import jax
import jax.numpy as jnp
from jax import lax
from jax.experimental import pallas as pl
from jax.experimental.pallas import tpu as pltpu
from jax.sharding import PartitionSpec as P

BLOCKS = 4
EDGE = 64
FREQS = 2
Y = 4
SHOT = 16
Z = 8
LANES = 128
MESH = pl.DeviceIdType.MESH


def taper_weights(columns, aperture_start, aperture_end, taper_bin, taper_gain):
    inside = (columns[None, :] >= aperture_start[:, None]) & (
        columns[None, :] < aperture_end[:, None]
    )
    distance = jnp.minimum(
        columns[None, :] - aperture_start[:, None], aperture_end[:, None] - 1 - columns[None, :]
    )
    ramped = jnp.minimum((distance + 1).astype(jnp.float32) / EDGE, 1.0)
    labels = jnp.arange(taper_gain.shape[0], dtype=jnp.int32)
    bin_gain = jnp.sum(
        jnp.where(taper_bin[:, None] == labels[None, :], taper_gain[None, :], 0.0), axis=1
    )
    return jnp.where(inside, ramped, 0.0) * bin_gain[None, :]


def chain_length(sign, part):
    return 4 if (sign > 0) == (part == 0) else 3


def kernel(
    owner_ref, rec_ref, t_ref, out_ref,
    a2a_0, a2a_1, selx, A, tp, L, own, zsend, zrecv,
    a_loc, a_send, a_recv, g_send, g_recv, p_send, p_recv, ag_send, ag_recv, z_send, z_recv,
):
    a2a = (a2a_0, a2a_1)
    me = lax.axis_index("shot")
    rb = lax.axis_index("rbin")
    core = lax.rem(me, 2)
    q = lax.div(me, 2)
    x_lo = lax.div(q, Y)
    y = lax.rem(q, Y)
    x_hi = lax.div(rb, Z)
    z = lax.rem(rb, Z)
    half = t_ref.shape[3] * 4

    def shot_of(xl, yy, cc):
        return (xl * Y + lax.rem(yy, Y)) * 2 + cc

    partner = {"rbin": (1 - x_hi) * Z + z}
    z_next = {1: {"rbin": x_hi * Z + lax.rem(z + 1, Z)}, -1: {"rbin": x_hi * Z + lax.rem(z + Z - 1, Z)}}
    other_core = {"shot": shot_of(x_lo, y, 1 - core)}
    x_other = {"shot": shot_of(1 - x_lo, y, core)}
    y_up = {"shot": shot_of(x_lo, y + 1, core)}
    y_down = {"shot": shot_of(x_lo, y + Y - 1, core)}

    barrier = pltpu.get_barrier_semaphore()

    def greet(k, carry):
        pl.semaphore_signal(
            barrier, inc=1, device_id={"shot": lax.rem(me + k, SHOT)}, device_id_type=MESH
        )
        return carry

    lax.fori_loop(1, SHOT, greet, 0)
    for target in (partner, z_next[1], z_next[-1]):
        pl.semaphore_signal(barrier, inc=1, device_id=target, device_id_type=MESH)
    pl.semaphore_wait(barrier, SHOT - 1 + 3)

    pending = []

    def remote(src, dst, send_sem, recv_sem, target):
        copy = pltpu.make_async_remote_copy(
            src_ref=src, dst_ref=dst, send_sem=send_sem, recv_sem=recv_sem,
            device_id=target, device_id_type=MESH,
        )
        copy.start()
        pending.append(copy)

    def arrived(ref, sem):
        pltpu.make_async_copy(ref, ref, sem).wait()

    def chunk(f, target, h):
        start = pl.multiple_of(h * half + lax.div(target, 2) * LANES, LANES)
        return rec_ref.at[0, f, lax.rem(target, 2), :, pl.ds(start, LANES)]

    def exchange_start(f):
        def body(k, carry):
            target = lax.rem(me + k, SHOT)
            for h in range(2):
                pltpu.make_async_remote_copy(
                    src_ref=chunk(f, target, h), dst_ref=a2a[f].at[me, h],
                    send_sem=a_send.at[f, h, k], recv_sem=a_recv.at[f, h, k],
                    device_id={"shot": target}, device_id_type=MESH,
                ).start()
            return carry

        lax.fori_loop(1, SHOT, body, 0)
        for h in range(2):
            pltpu.make_async_copy(chunk(f, me, h), a2a[f].at[me, h], a_loc.at[f, h]).start()

    def exchange_wait(f):
        def body(k, carry):
            source = lax.rem(me + SHOT - k, SHOT)
            for h in range(2):
                arrived(a2a[f].at[source, h], a_recv.at[f, h, k])
            return carry

        lax.fori_loop(1, SHOT, body, 0)
        for h in range(2):
            arrived(a2a[f].at[me, h], a_loc.at[f, h])

    def exchange_end(f):
        def body(k, carry):
            target = lax.rem(me + k, SHOT)
            for h in range(2):
                arrived(a2a[f].at[target, h], a_send.at[f, h, k])
            return carry

        lax.fori_loop(1, SHOT, body, 0)

    def gathers_start(f):
        remote(t_ref.at[f], tp.at[f], g_send.at[f], g_recv.at[f], partner)

    def select(f):
        for k in range(BLOCKS):
            owner = owner_ref[k]
            rows = pl.ds((k % 2) * 64, 64)
            selx[f, k // 2, rows, :] = a2a[f][owner, 1 - x_hi]
            A[f, q, core, 0, k // 2, rows, :] = a2a[f][owner, x_hi]
        remote(selx.at[f], A.at[f, q, core, 1], p_send.at[f], p_recv.at[f], partner)

    def at_chip(xl, yy):
        return xl * Y + lax.rem(yy, Y)

    pieces = [
        at_chip(1 - x_lo, y),
        at_chip(x_lo, y + Y - 1),
        at_chip(1 - x_lo, y + Y - 1),
        at_chip(x_lo, y + 1),
        at_chip(1 - x_lo, y + 1),
        at_chip(x_lo, y + 2),
        at_chip(1 - x_lo, y + 2),
    ]

    def ag_copy(f, b, index, piece, target):
        ref = A.at[f, piece, core, b]
        remote(ref, ref, ag_send.at[f, b, index], ag_recv.at[f, b, index], target)

    def ag_got(f, b, index):
        arrived(A.at[f, pieces[index], core, b], ag_recv.at[f, b, index])
        ag_copy(f, b, 8 + index, pieces[index], other_core)

    def ag_first(f, b):
        ag_copy(f, b, 0, q, x_other)
        ag_copy(f, b, 1, q, y_up)
        ag_copy(f, b, 3, q, y_down)
        ag_copy(f, b, 7, q, other_core)

    def ag_begin(f):
        ag_first(f, 0)
        arrived(A.at[f, q, core, 1], p_recv.at[f])
        ag_first(f, 1)

    def ag_second(f):
        for b in range(2):
            ag_got(f, b, 0)
            ag_copy(f, b, 2, pieces[0], y_up)
            ag_copy(f, b, 4, pieces[0], y_down)

    def ag_relay(f):
        for b in range(2):
            ag_got(f, b, 1)
            ag_copy(f, b, 5, pieces[1], y_up)
            ag_got(f, b, 4)
            ag_copy(f, b, 6, pieces[4], y_down)
            ag_got(f, b, 3)
            ag_got(f, b, 2)

    def ag_finish(f):
        for b in range(2):
            ag_got(f, b, 5)
            ag_got(f, b, 6)
        for b in range(2):
            arrived(A.at[f, q, 1 - core, b], ag_recv.at[f, b, 7])
            for index in range(7):
                arrived(A.at[f, pieces[index], 1 - core, b], ag_recv.at[f, b, 8 + index])

    width = t_ref.shape[3]

    def lhs(f):
        arrived(tp.at[f], g_recv.at[f])
        for b, ref in enumerate((t_ref, tp)):
            cols = [pl.ds(c * 2 * width + b * width, width) for c in range(2)]
            L[0, :, cols[0]] = ref[f, 0]
            L[0, :, cols[1]] = -ref[f, 1]
            L[1, :, cols[0]] = ref[f, 1]
            L[1, :, cols[1]] = ref[f, 0]

    def z_put(f, sign, part, step):
        i = 0 if sign > 0 else 1
        remote(
            zsend.at[f, i, part, step], zrecv.at[f, i, part, step],
            z_send.at[f, i, part, step], z_recv.at[f, i, part, step], z_next[sign],
        )

    def product(f, pair):
        right = jnp.concatenate(
            [A[f, lax.rem(z + d + Z, Z)].reshape(-1, LANES) for d in pair], axis=1
        )
        for part in range(2):
            value = jnp.dot(L[part], right, preferred_element_type=jnp.float32)
            for n, d in enumerate(pair):
                own[f, d % Z, part] = value[:, n * LANES:(n + 1) * LANES]

    def z_open(f):
        lhs(f)
        product(f, (4, 3))
        z_first(f, 1, 0)
        z_first(f, -1, 1)
        z_first(f, 1, 1)
        product(f, (-3, 2))
        z_first(f, -1, 0)
        product(f, (-2, 1))
        product(f, (-1, 0))

    def z_first(f, sign, part):
        i = 0 if sign > 0 else 1
        d = sign * chain_length(sign, part)
        zsend[f, i, part, 0] = own[f, d % Z, part].astype(jnp.bfloat16)
        z_put(f, sign, part, 0)

    def z_step(f, step):
        for sign, part in ((1, 0), (-1, 1), (1, 1), (-1, 0)):
            length = chain_length(sign, part)
            if step >= length:
                continue
            i = 0 if sign > 0 else 1
            arrived(zrecv.at[f, i, part, step - 1], z_recv.at[f, i, part, step - 1])
            d = sign * (length - step)
            zsend[f, i, part, step] = (
                zrecv[f, i, part, step - 1].astype(jnp.float32) + own[f, d % Z, part]
            ).astype(jnp.bfloat16)
            z_put(f, sign, part, step)

    def z_last(f):
        for part in range(2):
            total = own[f, 0, part]
            for i, sign in enumerate((1, -1)):
                last = chain_length(sign, part) - 1
                arrived(zrecv.at[f, i, part, last], z_recv.at[f, i, part, last])
                total = total + zrecv[f, i, part, last].astype(jnp.float32)
            out_ref[f, part] = total.T

    exchange_start(0)
    gathers_start(0)
    exchange_start(1)
    gathers_start(1)
    exchange_wait(0)
    select(0)
    ag_begin(0)
    ag_second(0)
    ag_relay(0)
    exchange_wait(1)
    select(1)
    ag_finish(0)
    z_open(0)
    ag_begin(1)
    z_step(0, 1)
    ag_second(1)
    z_step(0, 2)
    ag_relay(1)
    ag_finish(1)
    z_step(0, 3)
    z_open(1)
    z_last(0)
    for step in range(1, 4):
        z_step(1, step)
    z_last(1)
    for f in range(FREQS):
        exchange_end(f)
    for copy in pending:
        copy.wait_send()


def convolve(owner, recorded, tapered):
    freqs, _, shots, width = tapered.shape
    bf16, f32, dma = jnp.bfloat16, jnp.float32, pltpu.SemaphoreType.DMA
    return pl.pallas_call(
        kernel,
        out_shape=jax.ShapeDtypeStruct((freqs, 2, LANES, shots), f32),
        in_specs=[
            pl.BlockSpec(memory_space=pltpu.SMEM),
            pl.BlockSpec(memory_space=pl.ANY),
            pl.BlockSpec(memory_space=pltpu.VMEM),
        ],
        out_specs=pl.BlockSpec(memory_space=pltpu.VMEM),
        scratch_shapes=[
            pltpu.VMEM((SHOT, 2, 64, LANES), bf16),
            pltpu.VMEM((SHOT, 2, 64, LANES), bf16),
            pltpu.VMEM((freqs, 2, LANES, LANES), bf16),
            pltpu.VMEM((freqs, Z, 2, 2, 2, LANES, LANES), bf16),
            pltpu.VMEM((freqs, 2, shots, width), bf16),
            pltpu.VMEM((2, shots, 4 * width), bf16),
            pltpu.VMEM((freqs, Z, 2, shots, LANES), f32),
            pltpu.VMEM((freqs, 2, 2, 4, shots, LANES), bf16),
            pltpu.VMEM((freqs, 2, 2, 4, shots, LANES), bf16),
            dma((freqs, 2)),
            dma((freqs, 2, SHOT)),
            dma((freqs, 2, SHOT)),
            dma((freqs,)),
            dma((freqs,)),
            dma((freqs,)),
            dma((freqs,)),
            dma((freqs, 2, 15)),
            dma((freqs, 2, 15)),
            dma((freqs, 2, 2, 4)),
            dma((freqs, 2, 2, 4)),
        ],
        compiler_params=pltpu.CompilerParams(
            collective_id=0, has_side_effects=True, vmem_limit_bytes=48 * 1024 * 1024
        ),
        name="convolve",
    )(owner, recorded, tapered)


def per_device(
    local_gathers, recorded_shots, block_owner, aperture_start, aperture_end, taper_bin, taper_gain
):
    point_count = local_gathers.shape[3]
    columns = lax.axis_index("rbin") * point_count + jnp.arange(point_count, dtype=jnp.int32)
    weight = taper_weights(columns, aperture_start, aperture_end, taper_bin, taper_gain)
    tapered = -(local_gathers.astype(jnp.float32) * weight[None, None]).astype(jnp.bfloat16)
    return convolve(block_owner, recorded_shots, tapered).transpose(0, 2, 1, 3)


def solution(mesh):
    in_specs = (
        P(None, None, "shot", "rbin"),
        P("shot", None, None, "rbin", None),
        P(),
        P("shot"),
        P("shot"),
        P("rbin"),
        P(),
    )
    out_specs = P(None, "rbin", None, "shot")
    return jax.shard_map(
        per_device, mesh=mesh, in_specs=in_specs, out_specs=out_specs, check_vma=False
    )
```

```python
import jax
import jax.numpy as jnp
from jax import lax
from jax.experimental import pallas as pl
from jax.experimental.pallas import tpu as pltpu
from jax.sharding import PartitionSpec as P

BLOCKS = 4
EDGE = 64
FREQS = 2
Y = 4
SHOT = 16
Z = 8
LANES = 128
MESH = pl.DeviceIdType.MESH


def taper_weights(columns, aperture_start, aperture_end, taper_bin, taper_gain):
    inside = (columns[None, :] >= aperture_start[:, None]) & (
        columns[None, :] < aperture_end[:, None]
    )
    distance = jnp.minimum(
        columns[None, :] - aperture_start[:, None], aperture_end[:, None] - 1 - columns[None, :]
    )
    ramped = jnp.minimum((distance + 1).astype(jnp.float32) / EDGE, 1.0)
    labels = jnp.arange(taper_gain.shape[0], dtype=jnp.int32)
    bin_gain = jnp.sum(
        jnp.where(taper_bin[:, None] == labels[None, :], taper_gain[None, :], 0.0), axis=1
    )
    return jnp.where(inside, ramped, 0.0) * bin_gain[None, :]


def chain_length(sign, part):
    return 4 if (sign > 0) == (part == 0) else 3


def kernel(
    owner_ref, rec_ref, t_ref, out_ref,
    a2a_0, a2a_1, selx, A, tp, L, own, zsend, zrecv,
    a_loc, a_send, a_recv, g_send, g_recv, p_send, p_recv, ag_send, ag_recv, z_send, z_recv,
):
    a2a = (a2a_0, a2a_1)
    me = lax.axis_index("shot")
    rb = lax.axis_index("rbin")
    core = lax.rem(me, 2)
    q = lax.div(me, 2)
    x_lo = lax.div(q, Y)
    y = lax.rem(q, Y)
    x_hi = lax.div(rb, Z)
    z = lax.rem(rb, Z)
    half = t_ref.shape[3] * 4

    def shot_of(xl, yy, cc):
        return (xl * Y + lax.rem(yy, Y)) * 2 + cc

    partner = {"rbin": (1 - x_hi) * Z + z}
    z_next = {1: {"rbin": x_hi * Z + lax.rem(z + 1, Z)}, -1: {"rbin": x_hi * Z + lax.rem(z + Z - 1, Z)}}
    other_core = {"shot": shot_of(x_lo, y, 1 - core)}
    x_other = {"shot": shot_of(1 - x_lo, y, core)}
    y_up = {"shot": shot_of(x_lo, y + 1, core)}
    y_down = {"shot": shot_of(x_lo, y + Y - 1, core)}

    barrier = pltpu.get_barrier_semaphore()

    def greet(k, carry):
        pl.semaphore_signal(
            barrier, inc=1, device_id={"shot": lax.rem(me + k, SHOT)}, device_id_type=MESH
        )
        return carry

    lax.fori_loop(1, SHOT, greet, 0)
    for target in (partner, z_next[1], z_next[-1]):
        pl.semaphore_signal(barrier, inc=1, device_id=target, device_id_type=MESH)
    pl.semaphore_wait(barrier, SHOT - 1 + 3)

    pending = []

    def remote(src, dst, send_sem, recv_sem, target):
        copy = pltpu.make_async_remote_copy(
            src_ref=src, dst_ref=dst, send_sem=send_sem, recv_sem=recv_sem,
            device_id=target, device_id_type=MESH,
        )
        copy.start()
        pending.append(copy)

    def arrived(ref, sem):
        pltpu.make_async_copy(ref, ref, sem).wait()

    def chunk(f, target, h):
        start = pl.multiple_of(h * half + lax.div(target, 2) * LANES, LANES)
        return rec_ref.at[0, f, lax.rem(target, 2), :, pl.ds(start, LANES)]

    def exchange_start(f):
        def body(k, carry):
            target = lax.rem(me + k, SHOT)
            for h in range(2):
                pltpu.make_async_remote_copy(
                    src_ref=chunk(f, target, h), dst_ref=a2a[f].at[me, h],
                    send_sem=a_send.at[f, h, k], recv_sem=a_recv.at[f, h, k],
                    device_id={"shot": target}, device_id_type=MESH,
                ).start()
            return carry

        lax.fori_loop(1, SHOT, body, 0)
        for h in range(2):
            pltpu.make_async_copy(chunk(f, me, h), a2a[f].at[me, h], a_loc.at[f, h]).start()

    def exchange_wait(f):
        def body(k, carry):
            source = lax.rem(me + SHOT - k, SHOT)
            for h in range(2):
                arrived(a2a[f].at[source, h], a_recv.at[f, h, k])
            return carry

        lax.fori_loop(1, SHOT, body, 0)
        for h in range(2):
            arrived(a2a[f].at[me, h], a_loc.at[f, h])

    def exchange_end(f):
        def body(k, carry):
            target = lax.rem(me + k, SHOT)
            for h in range(2):
                arrived(a2a[f].at[target, h], a_send.at[f, h, k])
            return carry

        lax.fori_loop(1, SHOT, body, 0)

    def gathers_start(f):
        remote(t_ref.at[f], tp.at[f], g_send.at[f], g_recv.at[f], partner)

    def select(f):
        for k in range(BLOCKS):
            owner = owner_ref[k]
            rows = pl.ds((k % 2) * 64, 64)
            selx[f, k // 2, rows, :] = a2a[f][owner, 1 - x_hi]
            A[f, q, core, 0, k // 2, rows, :] = a2a[f][owner, x_hi]
        remote(selx.at[f], A.at[f, q, core, 1], p_send.at[f], p_recv.at[f], partner)

    def at_chip(xl, yy):
        return xl * Y + lax.rem(yy, Y)

    pieces = [
        at_chip(1 - x_lo, y),
        at_chip(x_lo, y + Y - 1),
        at_chip(1 - x_lo, y + Y - 1),
        at_chip(x_lo, y + 1),
        at_chip(1 - x_lo, y + 1),
        at_chip(x_lo, y + 2),
        at_chip(1 - x_lo, y + 2),
    ]

    def ag_copy(f, b, index, piece, target):
        ref = A.at[f, piece, core, b]
        remote(ref, ref, ag_send.at[f, b, index], ag_recv.at[f, b, index], target)

    def ag_got(f, b, index):
        arrived(A.at[f, pieces[index], core, b], ag_recv.at[f, b, index])
        ag_copy(f, b, 8 + index, pieces[index], other_core)

    def ag_first(f, b):
        ag_copy(f, b, 0, q, x_other)
        ag_copy(f, b, 1, q, y_up)
        ag_copy(f, b, 3, q, y_down)
        ag_copy(f, b, 7, q, other_core)

    def ag_begin(f):
        ag_first(f, 0)
        arrived(A.at[f, q, core, 1], p_recv.at[f])
        ag_first(f, 1)

    def ag_second(f):
        for b in range(2):
            ag_got(f, b, 0)
            ag_copy(f, b, 2, pieces[0], y_up)
            ag_copy(f, b, 4, pieces[0], y_down)

    def ag_relay(f):
        for b in range(2):
            ag_got(f, b, 1)
            ag_copy(f, b, 5, pieces[1], y_up)
            ag_got(f, b, 4)
            ag_copy(f, b, 6, pieces[4], y_down)
            ag_got(f, b, 3)
            ag_got(f, b, 2)

    def ag_finish(f):
        for b in range(2):
            ag_got(f, b, 5)
            ag_got(f, b, 6)
        for b in range(2):
            arrived(A.at[f, q, 1 - core, b], ag_recv.at[f, b, 7])
            for index in range(7):
                arrived(A.at[f, pieces[index], 1 - core, b], ag_recv.at[f, b, 8 + index])

    width = t_ref.shape[3]

    def lhs(f):
        arrived(tp.at[f], g_recv.at[f])
        for b, ref in enumerate((t_ref, tp)):
            cols = [pl.ds(c * 2 * width + b * width, width) for c in range(2)]
            L[0, :, cols[0]] = ref[f, 0]
            L[0, :, cols[1]] = -ref[f, 1]
            L[1, :, cols[0]] = ref[f, 1]
            L[1, :, cols[1]] = ref[f, 0]

    def z_put(f, sign, part, step):
        i = 0 if sign > 0 else 1
        remote(
            zsend.at[f, i, part, step], zrecv.at[f, i, part, step],
            z_send.at[f, i, part, step], z_recv.at[f, i, part, step], z_next[sign],
        )

    def product(f, pair):
        right = jnp.concatenate(
            [A[f, lax.rem(z + d + Z, Z)].reshape(-1, LANES) for d in pair], axis=1
        )
        for part in range(2):
            value = jnp.dot(L[part], right, preferred_element_type=jnp.float32)
            for n, d in enumerate(pair):
                own[f, d % Z, part] = value[:, n * LANES:(n + 1) * LANES]

    def z_open(f):
        lhs(f)
        product(f, (4, 3))
        z_first(f, 1, 0)
        z_first(f, -1, 1)
        z_first(f, 1, 1)
        product(f, (-3, 2))
        z_first(f, -1, 0)
        product(f, (-2, 1))
        product(f, (-1, 0))

    def z_first(f, sign, part):
        i = 0 if sign > 0 else 1
        d = sign * chain_length(sign, part)
        zsend[f, i, part, 0] = own[f, d % Z, part].astype(jnp.bfloat16)
        z_put(f, sign, part, 0)

    def z_step(f, step):
        for sign, part in ((1, 0), (-1, 1), (1, 1), (-1, 0)):
            length = chain_length(sign, part)
            if step >= length:
                continue
            i = 0 if sign > 0 else 1
            arrived(zrecv.at[f, i, part, step - 1], z_recv.at[f, i, part, step - 1])
            d = sign * (length - step)
            zsend[f, i, part, step] = (
                zrecv[f, i, part, step - 1].astype(jnp.float32) + own[f, d % Z, part]
            ).astype(jnp.bfloat16)
            z_put(f, sign, part, step)

    def z_last(f):
        for part in range(2):
            total = own[f, 0, part]
            for i, sign in enumerate((1, -1)):
                last = chain_length(sign, part) - 1
                arrived(zrecv.at[f, i, part, last], z_recv.at[f, i, part, last])
                total = total + zrecv[f, i, part, last].astype(jnp.float32)
            out_ref[f, part] = total.T

    exchange_start(0)
    gathers_start(0)
    exchange_wait(0)
    select(0)
    ag_begin(0)
    exchange_start(1)
    ag_second(0)
    ag_relay(0)
    gathers_start(1)
    ag_finish(0)
    z_open(0)
    exchange_wait(1)
    select(1)
    z_step(0, 1)
    ag_begin(1)
    ag_second(1)
    z_step(0, 2)
    ag_relay(1)
    z_step(0, 3)
    ag_finish(1)
    z_open(1)
    z_last(0)
    for step in range(1, 4):
        z_step(1, step)
    z_last(1)
    for f in range(FREQS):
        exchange_end(f)
    for copy in pending:
        copy.wait_send()


def convolve(owner, recorded, tapered):
    freqs, _, shots, width = tapered.shape
    bf16, f32, dma = jnp.bfloat16, jnp.float32, pltpu.SemaphoreType.DMA
    return pl.pallas_call(
        kernel,
        out_shape=jax.ShapeDtypeStruct((freqs, 2, LANES, shots), f32),
        in_specs=[
            pl.BlockSpec(memory_space=pltpu.SMEM),
            pl.BlockSpec(memory_space=pl.ANY),
            pl.BlockSpec(memory_space=pltpu.VMEM),
        ],
        out_specs=pl.BlockSpec(memory_space=pltpu.VMEM),
        scratch_shapes=[
            pltpu.VMEM((SHOT, 2, 64, LANES), bf16),
            pltpu.VMEM((SHOT, 2, 64, LANES), bf16),
            pltpu.VMEM((freqs, 2, LANES, LANES), bf16),
            pltpu.VMEM((freqs, Z, 2, 2, 2, LANES, LANES), bf16),
            pltpu.VMEM((freqs, 2, shots, width), bf16),
            pltpu.VMEM((2, shots, 4 * width), bf16),
            pltpu.VMEM((freqs, Z, 2, shots, LANES), f32),
            pltpu.VMEM((freqs, 2, 2, 4, shots, LANES), bf16),
            pltpu.VMEM((freqs, 2, 2, 4, shots, LANES), bf16),
            dma((freqs, 2)),
            dma((freqs, 2, SHOT)),
            dma((freqs, 2, SHOT)),
            dma((freqs,)),
            dma((freqs,)),
            dma((freqs,)),
            dma((freqs,)),
            dma((freqs, 2, 15)),
            dma((freqs, 2, 15)),
            dma((freqs, 2, 2, 4)),
            dma((freqs, 2, 2, 4)),
        ],
        compiler_params=pltpu.CompilerParams(
            collective_id=0, has_side_effects=True, vmem_limit_bytes=48 * 1024 * 1024
        ),
        name="convolve",
    )(owner, recorded, tapered)


def per_device(
    local_gathers, recorded_shots, block_owner, aperture_start, aperture_end, taper_bin, taper_gain
):
    point_count = local_gathers.shape[3]
    columns = lax.axis_index("rbin") * point_count + jnp.arange(point_count, dtype=jnp.int32)
    weight = taper_weights(columns, aperture_start, aperture_end, taper_bin, taper_gain)
    tapered = -(local_gathers.astype(jnp.float32) * weight[None, None]).astype(jnp.bfloat16)
    return convolve(block_owner, recorded_shots, tapered).transpose(0, 2, 1, 3)


def solution(mesh):
    in_specs = (
        P(None, None, "shot", "rbin"),
        P("shot", None, None, "rbin", None),
        P(),
        P("shot"),
        P("shot"),
        P("rbin"),
        P(),
    )
    out_specs = P(None, "rbin", None, "shot")
    return jax.shard_map(
        per_device, mesh=mesh, in_specs=in_specs, out_specs=out_specs, check_vma=False
    )
```
